32 devices in a mesh: group: 4 (over y, x), member: 8 (over z, core).
Axes of the slice: x: 2, y: 2, z: 4, core: 2. Of those that a mesh axis runs over, the one named last changes fastest.
Arguments:
- picture_embedding_matrix: bfloat16 [8192, 1152], P(('group', 'member')), may hold values from -1 to 1
- caption_embedding_matrix: bfloat16 [8192, 1152], P(('group', 'member')), may hold values from -1 to 1
- learned_sharpness: float32 [1], replicated, may hold values from 5 to 20
- learned_offset_entry: float32 [1], replicated, may hold values from -4 to -2
Outputs:
- grad_images: float32 [8192, 1152], P(('group', 'member'))
- grad_texts: float32 [8192, 1152], P(('group', 'member'))
The draws below stay inside these ranges and needn't reach their ends.
All inputs are finite; a program needn't handle non-finite values.
Results may differ from the reference program's by a relative error of at most 0.002.
Values may be sent and summed in bfloat16 or wider, within the bound.
A program may use at most 192 MiB of HBM per device.

```python
import math
import jax
import jax.numpy as jnp
from jax import lax

D = 1152
ROWS = 256
GROUP_ROWS = 2048
TOTAL = 8192
N_GROUP = 4
N_MEMBER = 8


def paired_rows(key):
    base_key = jax.random.fold_in(key, 7301)
    image_key, noise_key, ratio_key = jax.random.split(base_key, 3)
    spread = 1.0 / math.sqrt(D)
    picture_features = jnp.clip(spread * jax.random.normal(image_key, (TOTAL, D), jnp.float32), -5.0 * spread, 5.0 * spread)
    noise_rows = jnp.clip(spread * jax.random.normal(noise_key, (TOTAL, D), jnp.float32), -5.0 * spread, 5.0 * spread)
    pair_ratio = jax.random.uniform(ratio_key, (TOTAL, 1), jnp.float32, 0.15, 0.35)
    caption_features = pair_ratio * picture_features + jnp.sqrt(1.0 - pair_ratio * pair_ratio) * noise_rows
    caption_features = jnp.clip(caption_features, -1.0, 1.0)
    return (picture_features, caption_features)


def draw_picture_embedding_matrix(key, part):
    return paired_rows(key)[0].astype(jnp.bfloat16)


def draw_caption_embedding_matrix(key, part):
    return paired_rows(key)[1].astype(jnp.bfloat16)


def setup_inputs(seed: int = 0) -> dict:
    arg_keys = jax.random.split(jax.random.key(seed), 5)
    return {
        "picture_embedding_matrix": draw_picture_embedding_matrix(jax.random.fold_in(arg_keys[4], 71), 0),
        "caption_embedding_matrix": draw_caption_embedding_matrix(jax.random.fold_in(arg_keys[4], 71), 0),
        "learned_sharpness": jnp.clip(jnp.exp(jax.random.uniform(arg_keys[2], (1,), jnp.float32, math.log(5.0), math.log(20.0))), 5.0, 20.0),
        "learned_offset_entry": jnp.clip(jax.random.uniform(arg_keys[3], (1,), jnp.float32, -4.0, -2.0), -4.0, -2.0),
    }


def weighting_factors(similarity_scores, match_polarity, sharpness_multiplier):
    return (-sharpness_multiplier * match_polarity * jax.nn.sigmoid(-match_polarity * similarity_scores)).astype(jnp.bfloat16)


def reference(picture_embedding_matrix, caption_embedding_matrix, learned_sharpness, learned_offset_entry):
    sharpness_multiplier = learned_sharpness[0]
    offset_amount = learned_offset_entry[0]
    img_blocks = picture_embedding_matrix.reshape(N_GROUP, GROUP_ROWS, D)
    txt_blocks = caption_embedding_matrix.reshape(N_GROUP, GROUP_ROWS, D)
    txt_before = jnp.roll(txt_blocks, 1, axis=0)
    matching_polarity = jnp.eye(GROUP_ROWS, dtype=jnp.float32) * 2.0 - 1.0

    def one_group(block_groups):
        picture_features, caption_features, before = block_groups
        similarity_scores = sharpness_multiplier * jnp.dot(picture_features, caption_features.T, preferred_element_type=jnp.float32) + offset_amount
        score_multipliers = weighting_factors(similarity_scores, matching_polarity, sharpness_multiplier)
        grad_img = jnp.dot(score_multipliers, caption_features, preferred_element_type=jnp.float32)
        grad_txt = jnp.dot(score_multipliers.T, picture_features, preferred_element_type=jnp.float32)
        picture_participant = picture_features.reshape(N_MEMBER, ROWS, D).astype(jnp.float32)
        earlier_participant = before.reshape(N_MEMBER, ROWS, D).astype(jnp.float32)
        earlier_scores = sharpness_multiplier * jnp.einsum("eun,ean->eua", picture_participant, earlier_participant) + offset_amount
        earlier_multipliers = weighting_factors(earlier_scores, -1.0, sharpness_multiplier).astype(jnp.float32)
        grad_img = grad_img + jnp.einsum("mrs,msd->mrd", earlier_multipliers, earlier_participant).reshape(GROUP_ROWS, D)
        returned = jnp.einsum("mrs,mrd->msd", earlier_multipliers, picture_participant).reshape(GROUP_ROWS, D)
        return grad_img, grad_txt, returned

    grad_img, grad_txt, returned = lax.map(one_group, (img_blocks, txt_blocks, txt_before))
    grad_txt = grad_txt + jnp.roll(returned, -1, axis=0)
    return grad_img.reshape(TOTAL, D), grad_txt.reshape(TOTAL, D)
```

```python
import functools

import jax
import jax.numpy as jnp
from jax import lax
from jax.experimental import pallas as pl
from jax.experimental.pallas import tpu as pltpu
from jax.sharding import PartitionSpec as P

MESH = pl.DeviceIdType.MESH
F32 = jnp.float32
PIECES = 8
HOP = 4
AHEAD = 2
LAG = 1


def contract(a, b, da, db):
    return lax.dot_general(a, b, (((da,), (db,)), ((), ())), preferred_element_type=F32)


def order(i, k, n):
    own = jnp.minimum(HOP * k, PIECES)
    j = i - own
    far = (j >= 0) & (j < k * PIECES)
    text_b = jnp.where(far, j // PIECES, k)
    text_p = jnp.where(far, j % PIECES, jnp.where(j < 0, i, i - k * PIECES))
    near = jnp.where(k == 0, HOP, 0)
    i = i - (k + 1) * PIECES
    j, rest = i - near, (n - 2 - k) * PIECES
    far = (j >= 0) & (j < rest)
    sum_b = jnp.where(far, n - 1 - j // PIECES, k + 1)
    sum_p = jnp.where(far, j % PIECES, jnp.where(j < 0, i, i - rest))
    is_text = i < 0
    return is_text, jnp.where(is_text, text_b, sum_b), jnp.where(is_text, text_p, sum_p)


def kernel(
    groups, n, sharp_ref, bias_ref, img_hbm, txt_hbm, gi_ref, gt_ref,
    img_ref, other, gi_other, gi_in, txt_prev, img_next, tbuf, coef, gin, gout, vin, vout,
    t_send, t_recv, g_send, g_recv, v_send, v_recv, x_send, x_recv, l_sem,
):
    rows, width = img_ref.shape
    piece = rows // PIECES
    group = lax.axis_index("group")
    member = lax.axis_index("member")
    chip, core = member // 2, member % 2
    partner = (group, member + 1 - 2 * core)
    ahead = ((group + 1) % groups, member)
    behind = ((group + groups - 1) % groups, member)
    right, left = (group, member + 2), (group, member - 2)
    has_right, has_left = chip + 1 < n, chip > 0
    sharp, bias = sharp_ref[0], bias_ref[0]

    load_txt = pltpu.make_async_copy(txt_hbm, tbuf.at[chip], l_sem.at[0])
    load_img = pltpu.make_async_copy(img_hbm, img_ref, l_sem.at[1])
    load_txt.start()
    load_img.start()

    barrier = pltpu.get_barrier_semaphore()
    for device in (partner, ahead, behind):
        pl.semaphore_signal(barrier, inc=1, device_id=device, device_id_type=MESH)
    for exists, device in ((has_right, right), (has_left, left)):
        @pl.when(exists)
        def _():
            pl.semaphore_signal(barrier, inc=1, device_id=device, device_id_type=MESH)
    pl.semaphore_wait(barrier, 3 + has_right.astype(jnp.int32) + has_left.astype(jnp.int32))

    def remote(src, dst, send, recv, device):
        return pltpu.make_async_remote_copy(
            src_ref=src, dst_ref=dst, send_sem=send, recv_sem=recv,
            device_id=device, device_id_type=MESH,
        )

    def part_of(p):
        return pl.ds(pl.multiple_of(p * piece, piece), piece)

    def text(b, slot, p, device):
        block = tbuf.at[b, part_of(p)]
        return remote(block, block, t_send.at[slot, p], t_recv.at[b, p], device)

    def sums(b, slot, p, device):
        return remote(gout.at[b, p], gin.at[slot, p], g_send.at[b, p], g_recv.at[slot, p], device)

    def means(b, slot, p, device):
        return remote(vout.at[b, p], vin.at[slot, p], v_send.at[b, p], v_recv.at[slot, p], device)

    swap = remote(img_ref, other, x_send.at[0], x_recv.at[0], partner)
    to_ahead = remote(tbuf.at[chip], txt_prev, x_send.at[1], x_recv.at[1], ahead)
    to_behind = remote(img_ref, img_next, x_send.at[2], x_recv.at[2], behind)
    give = remote(gi_other, gi_in, x_send.at[3], x_recv.at[3], partner)

    sides = (
        (chip, has_right, right, chip, n),
        (n - 1 - chip, has_left, left, n, chip),
    )

    def seen(side, b):
        return b if side == 0 else n - 1 - b

    load_txt.wait()
    for k, more, onward, own_slot, _ in sides:
        @pl.when(more)
        def _():
            for p in range(HOP):
                text(chip, own_slot, p, onward).start()
    load_img.wait()
    swap.start()
    to_ahead.start()
    to_behind.start()

    def weights(dots, matching):
        logits = sharp * dots + bias
        if matching:
            hit = lax.broadcasted_iota(jnp.int32, dots.shape, 0) == lax.broadcasted_iota(
                jnp.int32, dots.shape, 1
            )
            sign = jnp.where(hit, 1.0, -1.0).astype(F32)
            return (-sign * (sharp / (1.0 + jnp.exp(sign * logits)))).astype(jnp.bfloat16)
        return (sharp / (1.0 + jnp.exp(-logits))).astype(jnp.bfloat16)

    def weigh(b, part):
        for half, img in ((0, img_ref), (1, other)):
            coef[b, half, part, :] = weights(contract(tbuf[b, part, :], img[...], 1, 1), False)

    def add_images(b):
        for half, total in ((0, gi_ref), (1, gi_other)):
            total[...] += contract(coef[b, half], tbuf[b], 0, 0)

    def share(b, p):
        part = part_of(p)
        return contract(coef[b, 0, part, :], img_ref[...], 1, 0) + contract(
            coef[b, 1, part, :], other[...], 1, 0
        )

    def send_on(b, slot, p, total, mean, device):
        middle = jnp.mean(total, axis=0, keepdims=True)
        gout[b, p] = (total - middle).astype(jnp.bfloat16)
        vout[b, p] = middle if mean is None else middle + mean
        sums(b, slot, p, device).start()
        means(b, slot, p, device).start()

    def arrived(slot, p):
        sums(0, slot, p, partner).wait_recv()
        means(0, slot, p, partner).wait_recv()

    own = tbuf.at[chip]
    c = weights(contract(own[...], img_ref[...], 1, 1), True)
    gi_ref[...] = contract(c, own[...], 0, 0)
    gt_ref[...] = contract(c, img_ref[...], 1, 0)
    swap.wait()
    c = weights(contract(own[...], other[...], 1, 1), False)
    gi_other[...] = contract(c, own[...], 0, 0)
    gt_ref[...] += contract(c, other[...], 1, 0)

    total_pieces = n * PIECES
    window_at = (n - 1) * PIECES - 1
    give_at = (n - 1) * PIECES + LAG
    take_at = total_pieces - 2

    @pl.loop(0, total_pieces + LAG)
    def _(s):
        for side, (k, more, onward, own_slot, home) in enumerate(sides):
            i, j = s + AHEAD, s - LAG
            out_text, out_b, out_p = order(i, k, n)
            in_text, in_b, in_p = order(j, k - 1, n)
            out_b, in_b = seen(side, out_b), seen(side, in_b)
            going = more & (i < total_pieces)
            coming = (k > 0) & (j >= 0)

            @pl.when(going & out_text & (out_b == chip) & (i >= HOP))
            def _():
                text(chip, own_slot, out_p, onward).start()

            b, p = jnp.where(more, out_b, in_b), jnp.where(more, out_p, in_p)

            @pl.when((going & out_text & (out_b != chip)) | (jnp.logical_not(more) & coming & in_text))
            def _():
                text(b, b, p, onward).wait_recv()

                @pl.when(more)
                def _():
                    text(b, b, p, onward).start()

                weigh(b, part_of(p))

                @pl.when(p == PIECES - 1)
                def _():
                    add_images(b)

            @pl.when(going & jnp.logical_not(out_text))
            def _():
                arrives_at = chip + 1 - 2 * side
                slot = jnp.where(out_b == arrives_at, n if side == 0 else out_b, out_b)
                here = share(out_b, out_p)

                @pl.when(k == 0)
                def _():
                    send_on(out_b, slot, out_p, here, None, onward)

                @pl.when(k > 0)
                def _():
                    arrived(out_b, out_p)
                    send_on(
                        out_b, slot, out_p, here + gin[out_b, out_p].astype(F32), vin[out_b, out_p], onward
                    )

            @pl.when(coming & jnp.logical_not(in_text) & (in_b == chip))
            def _():
                arrived(home, in_p)
                gt_ref[part_of(in_p), :] += gin[home, in_p].astype(F32) + vin[home, in_p]

        @pl.when(s == window_at)
        def _():
            to_ahead.wait_recv()
            c = weights(contract(img_ref[...], txt_prev[...], 1, 1), False)
            gi_ref[...] += contract(c, txt_prev[...], 1, 0)
            to_behind.wait_recv()
            c = weights(contract(own[...], img_next[...], 1, 1), False)
            gt_ref[...] += contract(c, img_next[...], 1, 0)

        @pl.when(s == give_at)
        def _():
            give.start()

        @pl.when(s == take_at)
        def _():
            give.wait_recv()
            gi_ref[...] += gi_in[...]

    give.wait_send()
    to_ahead.wait_send()
    to_behind.wait_send()

    @pl.loop(0, PIECES)
    def _(p):
        @pl.when(has_right)
        def _():
            text(chip, chip, p, right).wait_send()

        @pl.when(has_left)
        def _():
            text(chip, n, p, left).wait_send()

        @pl.loop(0, n)
        def _(b):
            @pl.when(((b < chip) & has_right) | ((b > chip) & has_left))
            def _():
                text(b, b, p, partner).wait_send()

            @pl.when(b != chip)
            def _():
                sums(b, b, p, partner).wait_send()
                means(b, b, p, partner).wait_send()


def solution(mesh):
    groups, members = mesh.shape["group"], mesh.shape["member"]
    n = members // 2

    def shards(images, texts, sharpness, offset):
        rows, width = images.shape
        piece = rows // PIECES
        bf16 = jnp.bfloat16
        out = jax.ShapeDtypeStruct((rows, width), F32)
        vmem = pl.BlockSpec(memory_space=pltpu.VMEM)
        smem = pl.BlockSpec(memory_space=pltpu.SMEM)
        hbm = pl.BlockSpec(memory_space=pltpu.HBM)
        dma = pltpu.SemaphoreType.DMA
        return pl.pallas_call(
            functools.partial(kernel, groups, n),
            out_shape=(out, out),
            in_specs=[smem, smem, hbm, hbm],
            out_specs=(vmem, vmem),
            scratch_shapes=[
                pltpu.VMEM((rows, width), bf16),
                pltpu.VMEM((rows, width), bf16),
                pltpu.VMEM((rows, width), F32),
                pltpu.VMEM((rows, width), F32),
                pltpu.VMEM((rows, width), bf16),
                pltpu.VMEM((rows, width), bf16),
                pltpu.VMEM((n, rows, width), bf16),
                pltpu.VMEM((n, 2, rows, rows), bf16),
                pltpu.VMEM((n + 1, PIECES, piece, width), bf16),
                pltpu.VMEM((n, PIECES, piece, width), bf16),
                pltpu.VMEM((n + 1, PIECES, 1, width), F32),
                pltpu.VMEM((n, PIECES, 1, width), F32),
                dma((n + 1, PIECES)),
                dma((n, PIECES)),
                dma((n, PIECES)),
                dma((n + 1, PIECES)),
                dma((n, PIECES)),
                dma((n + 1, PIECES)),
                dma((4,)),
                dma((4,)),
                dma((2,)),
            ],
            compiler_params=pltpu.CompilerParams(
                collective_id=0, has_side_effects=True, vmem_limit_bytes=min(60, 16 + 3 * n) * 1024 * 1024
            ),
        )(sharpness, offset, images, texts)

    spec = P(("group", "member"), None)
    return jax.shard_map(
        shards, mesh=mesh, in_specs=(spec, spec, P(), P()), out_specs=(spec, spec), check_vma=False
    )
```

```python
import functools

import jax
import jax.numpy as jnp
from jax import lax
from jax.experimental import pallas as pl
from jax.experimental.pallas import tpu as pltpu
from jax.sharding import PartitionSpec as P

MESH = pl.DeviceIdType.MESH
F32 = jnp.float32
PIECES = 8
HOP = 4
AHEAD = 2
LAG = 1


def contract(a, b, da, db):
    return lax.dot_general(a, b, (((da,), (db,)), ((), ())), preferred_element_type=F32)


def order(i, k, n):
    own = jnp.minimum(HOP * k, PIECES)
    j = i - own
    far = (j >= 0) & (j < k * PIECES)
    text_b = jnp.where(far, j // PIECES, k)
    text_p = jnp.where(far, j % PIECES, jnp.where(j < 0, i, i - k * PIECES))
    near = jnp.where(k == 0, HOP, 0)
    i = i - (k + 1) * PIECES
    j, rest = i - near, (n - 2 - k) * PIECES
    far = (j >= 0) & (j < rest)
    sum_b = jnp.where(far, n - 1 - j // PIECES, k + 1)
    sum_p = jnp.where(far, j % PIECES, jnp.where(j < 0, i, i - rest))
    is_text = i < 0
    return is_text, jnp.where(is_text, text_b, sum_b), jnp.where(is_text, text_p, sum_p)


def kernel(
    groups, n, sharp_ref, bias_ref, img_hbm, txt_hbm, gi_ref, gt_ref,
    img_ref, other, gi_other, gi_in, txt_prev, img_next, tbuf, coef, gin, gout, vin, vout,
    t_send, t_recv, g_send, g_recv, v_send, v_recv, x_send, x_recv, l_sem,
):
    rows, width = img_ref.shape
    piece = rows // PIECES
    group = lax.axis_index("group")
    member = lax.axis_index("member")
    chip, core = member // 2, member % 2
    partner = (group, member + 1 - 2 * core)
    ahead = ((group + 1) % groups, member)
    behind = ((group + groups - 1) % groups, member)
    right, left = (group, member + 2), (group, member - 2)
    has_right, has_left = chip + 1 < n, chip > 0
    sharp, bias = sharp_ref[0], bias_ref[0]

    load_txt = pltpu.make_async_copy(txt_hbm, tbuf.at[chip], l_sem.at[0])
    load_img = pltpu.make_async_copy(img_hbm, img_ref, l_sem.at[1])
    load_txt.start()
    load_img.start()

    barrier = pltpu.get_barrier_semaphore()
    for device in (partner, ahead, behind):
        pl.semaphore_signal(barrier, inc=1, device_id=device, device_id_type=MESH)
    for exists, device in ((has_right, right), (has_left, left)):
        @pl.when(exists)
        def _():
            pl.semaphore_signal(barrier, inc=1, device_id=device, device_id_type=MESH)
    pl.semaphore_wait(barrier, 3 + has_right.astype(jnp.int32) + has_left.astype(jnp.int32))

    def remote(src, dst, send, recv, device):
        return pltpu.make_async_remote_copy(
            src_ref=src, dst_ref=dst, send_sem=send, recv_sem=recv,
            device_id=device, device_id_type=MESH,
        )

    def part_of(p):
        return pl.ds(pl.multiple_of(p * piece, piece), piece)

    def text(b, slot, p, device):
        block = tbuf.at[b, part_of(p)]
        return remote(block, block, t_send.at[slot], t_recv.at[b, p], device)

    def sums(b, slot, p, device):
        return remote(gout.at[b, p], gin.at[slot, p], g_send.at[b], g_recv.at[slot, p], device)

    def means(b, slot, p, device):
        return remote(vout.at[b, p], vin.at[slot, p], v_send.at[b], v_recv.at[slot, p], device)

    swap = remote(img_ref, other, x_send.at[0], x_recv.at[0], partner)
    to_ahead = remote(tbuf.at[chip], txt_prev, x_send.at[1], x_recv.at[1], ahead)
    to_behind = remote(img_ref, img_next, x_send.at[2], x_recv.at[2], behind)
    give = remote(gi_other, gi_in, x_send.at[3], x_recv.at[3], partner)

    sides = (
        (chip, has_right, right, chip, n),
        (n - 1 - chip, has_left, left, n, chip),
    )

    def seen(side, b):
        return b if side == 0 else n - 1 - b

    load_txt.wait()
    for k, more, onward, own_slot, _ in sides:
        @pl.when(more)
        def _():
            for p in range(HOP):
                text(chip, own_slot, p, onward).start()
    load_img.wait()
    swap.start()
    to_ahead.start()
    to_behind.start()

    def weights(dots, matching):
        logits = sharp * dots + bias
        if matching:
            hit = lax.broadcasted_iota(jnp.int32, dots.shape, 0) == lax.broadcasted_iota(
                jnp.int32, dots.shape, 1
            )
            sign = jnp.where(hit, 1.0, -1.0).astype(F32)
            return (-sign * (sharp / (1.0 + jnp.exp(sign * logits)))).astype(jnp.bfloat16)
        return (sharp / (1.0 + jnp.exp(-logits))).astype(jnp.bfloat16)

    def weigh(b, part):
        for half, img in ((0, img_ref), (1, other)):
            coef[b, half, part, :] = weights(contract(tbuf[b, part, :], img[...], 1, 1), False)

    def add_images(b):
        for half, total in ((0, gi_ref), (1, gi_other)):
            total[...] += contract(coef[b, half], tbuf[b], 0, 0)

    def share(b, p):
        part = part_of(p)
        return contract(coef[b, 0, part, :], img_ref[...], 1, 0) + contract(
            coef[b, 1, part, :], other[...], 1, 0
        )

    def send_on(b, slot, p, total, mean, device):
        middle = jnp.mean(total, axis=0, keepdims=True)
        gout[b, p] = (total - middle).astype(jnp.bfloat16)
        vout[b, p] = middle if mean is None else middle + mean
        sums(b, slot, p, device).start()
        means(b, slot, p, device).start()

    def arrived(slot, p):
        sums(0, slot, p, partner).wait_recv()
        means(0, slot, p, partner).wait_recv()

    own = tbuf.at[chip]
    c = weights(contract(own[...], img_ref[...], 1, 1), True)
    gi_ref[...] = contract(c, own[...], 0, 0)
    gt_ref[...] = contract(c, img_ref[...], 1, 0)
    swap.wait()
    c = weights(contract(own[...], other[...], 1, 1), False)
    gi_other[...] = contract(c, own[...], 0, 0)
    gt_ref[...] += contract(c, other[...], 1, 0)

    total_pieces = n * PIECES
    window_at = (n - 1) * PIECES - 1
    give_at = (n - 1) * PIECES + LAG
    take_at = total_pieces - 2

    @pl.loop(0, total_pieces + LAG)
    def _(s):
        for side, (k, more, onward, own_slot, home) in enumerate(sides):
            i, j = s + AHEAD, s - LAG
            out_text, out_b, out_p = order(i, k, n)
            in_text, in_b, in_p = order(j, k - 1, n)
            out_b, in_b = seen(side, out_b), seen(side, in_b)
            going = more & (i < total_pieces)
            coming = (k > 0) & (j >= 0)

            @pl.when(going & out_text & (out_b == chip) & (i >= HOP))
            def _():
                text(chip, own_slot, out_p, onward).start()

            b, p = jnp.where(more, out_b, in_b), jnp.where(more, out_p, in_p)

            @pl.when((going & out_text & (out_b != chip)) | (jnp.logical_not(more) & coming & in_text))
            def _():
                text(b, b, p, onward).wait_recv()

                @pl.when(more)
                def _():
                    text(b, b, p, onward).start()

                weigh(b, part_of(p))

                @pl.when(p == PIECES - 1)
                def _():
                    add_images(b)

            @pl.when(going & jnp.logical_not(out_text))
            def _():
                arrives_at = chip + 1 - 2 * side
                slot = jnp.where(out_b == arrives_at, n if side == 0 else out_b, out_b)
                here = share(out_b, out_p)

                @pl.when(k == 0)
                def _():
                    send_on(out_b, slot, out_p, here, None, onward)

                @pl.when(k > 0)
                def _():
                    arrived(out_b, out_p)
                    send_on(
                        out_b, slot, out_p, here + gin[out_b, out_p].astype(F32), vin[out_b, out_p], onward
                    )

            @pl.when(coming & jnp.logical_not(in_text) & (in_b == chip))
            def _():
                arrived(home, in_p)
                gt_ref[part_of(in_p), :] += gin[home, in_p].astype(F32) + vin[home, in_p]

        @pl.when(s == window_at)
        def _():
            to_ahead.wait_recv()
            c = weights(contract(img_ref[...], txt_prev[...], 1, 1), False)
            gi_ref[...] += contract(c, txt_prev[...], 1, 0)
            to_behind.wait_recv()
            c = weights(contract(own[...], img_next[...], 1, 1), False)
            gt_ref[...] += contract(c, img_next[...], 1, 0)

        @pl.when(s == give_at)
        def _():
            give.start()

        @pl.when(s == take_at)
        def _():
            give.wait_recv()
            gi_ref[...] += gi_in[...]
            give.wait_send()
            to_ahead.wait_send()
            to_behind.wait_send()

            def all_text(b, slot):
                remote(tbuf.at[b], tbuf.at[b], t_send.at[slot], t_recv.at[b, 0], partner).wait_send()

            for _, more, _, own_slot, _ in sides:
                @pl.when(more)
                def _():
                    all_text(chip, own_slot)

            @pl.loop(0, n)
            def _(b):
                @pl.when(((b < chip) & has_right) | ((b > chip) & has_left))
                def _():
                    all_text(b, b)

    @pl.loop(0, n)
    def _(b):
        @pl.when(b != chip)
        def _():
            remote(gout.at[b], gout.at[b], g_send.at[b], g_recv.at[b, 0], partner).wait_send()
            remote(vout.at[b], vout.at[b], v_send.at[b], v_recv.at[b, 0], partner).wait_send()


def write_out(gi_ref, gt_ref, gi_out, gt_out, sem):
    copies = [
        pltpu.make_async_copy(gi_ref, gi_out, sem.at[0]),
        pltpu.make_async_copy(gt_ref, gt_out, sem.at[1]),
    ]
    for copy in copies:
        copy.start()
    for copy in copies:
        copy.wait()


def solution(mesh):
    groups, members = mesh.shape["group"], mesh.shape["member"]
    n = members // 2

    def shards(images, texts, sharpness, offset):
        rows, width = images.shape
        piece = rows // PIECES
        bf16 = jnp.bfloat16
        out = jax.ShapeDtypeStruct((rows, width), F32)
        vmem = pl.BlockSpec(memory_space=pltpu.VMEM)
        smem = pl.BlockSpec(memory_space=pltpu.SMEM)
        hbm = pl.BlockSpec(memory_space=pltpu.HBM)
        dma = pltpu.SemaphoreType.DMA
        gi, gt = pl.pallas_call(
            functools.partial(kernel, groups, n),
            out_shape=(out, out),
            in_specs=[smem, smem, hbm, hbm],
            out_specs=(vmem, vmem),
            scratch_shapes=[
                pltpu.VMEM((rows, width), bf16),
                pltpu.VMEM((rows, width), bf16),
                pltpu.VMEM((rows, width), F32),
                pltpu.VMEM((rows, width), F32),
                pltpu.VMEM((rows, width), bf16),
                pltpu.VMEM((rows, width), bf16),
                pltpu.VMEM((n, rows, width), bf16),
                pltpu.VMEM((n, 2, rows, rows), bf16),
                pltpu.VMEM((n + 1, PIECES, piece, width), bf16),
                pltpu.VMEM((n, PIECES, piece, width), bf16),
                pltpu.VMEM((n + 1, PIECES, 1, width), F32),
                pltpu.VMEM((n, PIECES, 1, width), F32),
                dma((n + 1,)),
                dma((n, PIECES)),
                dma((n,)),
                dma((n + 1, PIECES)),
                dma((n,)),
                dma((n + 1, PIECES)),
                dma((4,)),
                dma((4,)),
                dma((2,)),
            ],
            compiler_params=pltpu.CompilerParams(
                collective_id=0, has_side_effects=True, vmem_limit_bytes=min(60, 16 + 3 * n) * 1024 * 1024
            ),
        )(sharpness, offset, *(pltpu.with_memory_space_constraint(a, pltpu.HBM) for a in (images, texts)))
        return pl.pallas_call(
            write_out,
            out_shape=(out, out),
            in_specs=[vmem, vmem],
            out_specs=(hbm, hbm),
            scratch_shapes=[dma((2,))],
            compiler_params=pltpu.CompilerParams(vmem_limit_bytes=8 * 1024 * 1024),
        )(gi, gt)

    spec = P(("group", "member"), None)
    return jax.shard_map(
        shards, mesh=mesh, in_specs=(spec, spec, P(), P()), out_specs=(spec, spec), check_vma=False
    )
```

```python
import functools

import jax
import jax.numpy as jnp
from jax import lax
from jax.experimental import pallas as pl
from jax.experimental.pallas import tpu as pltpu
from jax.sharding import PartitionSpec as P

MESH = pl.DeviceIdType.MESH
F32 = jnp.float32
PIECES = 8
TALL = 1
WRITES = 4
HOP = 4
AHEAD = 2
LAG = 1


def contract(a, b, da, db):
    return lax.dot_general(a, b, (((da,), (db,)), ((), ())), preferred_element_type=F32)


def order(i, k, n):
    own = jnp.minimum(HOP * k, PIECES)
    j = i - own
    far = (j >= 0) & (j < k * PIECES)
    text_b = jnp.where(far, j // PIECES, k)
    text_p = jnp.where(far, j % PIECES, jnp.where(j < 0, i, i - k * PIECES))
    near = jnp.where(k == 0, HOP, 0)
    i = i - (k + 1) * PIECES
    j, rest = i - near, (n - 2 - k) * PIECES
    far = (j >= 0) & (j < rest)
    sum_b = jnp.where(far, n - 1 - j // PIECES, k + 1)
    sum_p = jnp.where(far, j % PIECES, jnp.where(j < 0, i, i - rest))
    is_text = i < 0
    return is_text, jnp.where(is_text, text_b, sum_b), jnp.where(is_text, text_p, sum_p)


def kernel(
    groups, n, sharp_ref, bias_ref, img_hbm, txt_hbm, gi_ref, gt_ref,
    img_ref, other, gi_other, gi_in, txt_prev, img_next, tbuf, coef, gin, gout, vin, vout,
    t_send, t_recv, g_send, g_recv, v_send, v_recv, x_send, x_recv, l_sem,
):
    rows, width = img_ref.shape
    piece = rows // PIECES
    group = lax.axis_index("group")
    member = lax.axis_index("member")
    chip, core = member // 2, member % 2
    partner = (group, member + 1 - 2 * core)
    ahead = ((group + 1) % groups, member)
    behind = ((group + groups - 1) % groups, member)
    right, left = (group, member + 2), (group, member - 2)
    has_right, has_left = chip + 1 < n, chip > 0

    load_txt = pltpu.make_async_copy(txt_hbm, tbuf.at[chip], l_sem.at[0])
    load_img = pltpu.make_async_copy(img_hbm, img_ref, l_sem.at[1])
    load_txt.start()
    load_img.start()

    barrier = pltpu.get_barrier_semaphore()
    for device in (partner, ahead, behind):
        pl.semaphore_signal(barrier, inc=1, device_id=device, device_id_type=MESH)
    for exists, device in ((has_right, right), (has_left, left)):
        @pl.when(exists)
        def _():
            pl.semaphore_signal(barrier, inc=1, device_id=device, device_id_type=MESH)
    pl.semaphore_wait(barrier, 3 + has_right.astype(jnp.int32) + has_left.astype(jnp.int32))

    def remote(src, dst, send, recv, device):
        return pltpu.make_async_remote_copy(
            src_ref=src, dst_ref=dst, send_sem=send, recv_sem=recv,
            device_id=device, device_id_type=MESH,
        )

    def part_of(p):
        return pl.ds(pl.multiple_of(p * piece, piece), piece)

    def text(b, slot, p, device):
        block = tbuf.at[b, part_of(p)]
        return remote(block, block, t_send.at[slot], t_recv.at[b, p], device)

    def sums(b, slot, p, device):
        return remote(gout.at[b, p], gin.at[slot, p], g_send.at[b], g_recv.at[slot, p], device)

    def means(b, slot, p, device):
        return remote(vout.at[b, p], vin.at[slot, p], v_send.at[b], v_recv.at[slot, p], device)

    swap = remote(img_ref, other, x_send.at[0], x_recv.at[0], partner)
    to_ahead = remote(tbuf.at[chip], txt_prev, x_send.at[1], x_recv.at[1], ahead)
    to_behind = remote(img_ref, img_next, x_send.at[2], x_recv.at[2], behind)
    give = remote(gi_other, gi_in, x_send.at[3], x_recv.at[3], partner)

    sides = (
        (chip, has_right, right, chip, n),
        (n - 1 - chip, has_left, left, n, chip),
    )

    def seen(side, b):
        return b if side == 0 else n - 1 - b

    load_txt.wait()
    for k, more, onward, own_slot, _ in sides:
        @pl.when(more)
        def _():
            for p in range(HOP):
                text(chip, own_slot, p, onward).start()
    load_img.wait()
    swap.start()
    to_ahead.start()
    to_behind.start()
    sharp, bias = sharp_ref[0], bias_ref[0]

    def weights(dots, matching):
        logits = sharp * dots + bias
        if matching:
            hit = lax.broadcasted_iota(jnp.int32, dots.shape, 0) == lax.broadcasted_iota(
                jnp.int32, dots.shape, 1
            )
            sign = jnp.where(hit, 1.0, -1.0).astype(F32)
            return (-sign * (sharp / (1.0 + jnp.exp(sign * logits)))).astype(jnp.bfloat16)
        return (sharp / (1.0 + jnp.exp(-logits))).astype(jnp.bfloat16)

    def weigh(b, part):
        for half, img in ((0, img_ref), (1, other)):
            coef[b, half, part, :] = weights(contract(tbuf[b, part, :], img[...], 1, 1), False)

    def add_images(b):
        for half, total in ((0, gi_ref), (1, gi_other)):
            total[...] += contract(coef[b, half], tbuf[b], 0, 0)

    def tall_part_of(q):
        return pl.ds(pl.multiple_of(q * TALL * piece, TALL * piece), TALL * piece)

    def share(b, q):
        part = tall_part_of(q)
        return contract(coef[b, 0, part, :], img_ref[...], 1, 0) + contract(
            coef[b, 1, part, :], other[...], 1, 0
        )

    def send_on(b, slot, p, total, mean, device):
        middle = jnp.mean(total, axis=0, keepdims=True)
        gout[b, p] = (total - middle).astype(jnp.bfloat16)
        vout[b, p] = middle if mean is None else middle + mean
        sums(b, slot, p, device).start()
        means(b, slot, p, device).start()

    def arrived(slot, p):
        sums(0, slot, p, partner).wait_recv()
        means(0, slot, p, partner).wait_recv()

    own = tbuf.at[chip]
    c = weights(contract(own[...], img_ref[...], 1, 1), True)
    gi_ref[...] = contract(c, own[...], 0, 0)
    gt_ref[...] = contract(c, img_ref[...], 1, 0)
    swap.wait()
    c = weights(contract(own[...], other[...], 1, 1), False)
    gi_other[...] = contract(c, own[...], 0, 0)
    gt_ref[...] += contract(c, other[...], 1, 0)

    def all_sums(b):
        remote(gout.at[b], gout.at[b], g_send.at[b], g_recv.at[b, 0], partner).wait_send()
        remote(vout.at[b], vout.at[b], v_send.at[b], v_recv.at[b, 0], partner).wait_send()

    total_pieces = n * PIECES
    window_at = (n - 1) * PIECES - 1
    give_at = (n - 1) * PIECES + LAG
    take_at = total_pieces - 2

    @pl.loop(0, total_pieces + LAG)
    def _(s):
        for side, (k, more, onward, own_slot, home) in enumerate(sides):
            i, j = s + AHEAD, s - LAG
            out_text, out_b, out_p = order(i, k, n)
            in_text, in_b, in_p = order(j, k - 1, n)
            out_b, in_b = seen(side, out_b), seen(side, in_b)
            going = more & (i < total_pieces)
            coming = (k > 0) & (j >= 0)

            @pl.when(going & out_text & (out_b == chip) & (i >= HOP))
            def _():
                text(chip, own_slot, out_p, onward).start()

            b, p = jnp.where(more, out_b, in_b), jnp.where(more, out_p, in_p)

            @pl.when((going & out_text & (out_b != chip)) | (jnp.logical_not(more) & coming & in_text))
            def _():
                text(b, b, p, onward).wait_recv()

                @pl.when(more)
                def _():
                    text(b, b, p, onward).start()

                weigh(b, part_of(p))

                @pl.when(p == PIECES - 1)
                def _():
                    add_images(b)

            @pl.when(going & jnp.logical_not(out_text) & (out_p % TALL == TALL - 1))
            def _():
                q = out_p // TALL
                arrives_at = chip + 1 - 2 * side
                slot = jnp.where(out_b == arrives_at, n if side == 0 else out_b, out_b)
                here = share(out_b, q)

                @pl.when(k == 0)
                def _():
                    send_on(out_b, slot, q, here, None, onward)

                @pl.when(k > 0)
                def _():
                    arrived(out_b, q)
                    send_on(out_b, slot, q, here + gin[out_b, q].astype(F32), vin[out_b, q], onward)

            @pl.when(coming & jnp.logical_not(in_text) & (in_b == chip) & (in_p % TALL == TALL - 1))
            def _():
                q = in_p // TALL
                arrived(home, q)
                gt_ref[tall_part_of(q), :] += gin[home, q].astype(F32) + vin[home, q]

        @pl.when(s == window_at)
        def _():
            to_ahead.wait_recv()
            c = weights(contract(img_ref[...], txt_prev[...], 1, 1), False)
            gi_ref[...] += contract(c, txt_prev[...], 1, 0)
            to_behind.wait_recv()
            c = weights(contract(own[...], img_next[...], 1, 1), False)
            gt_ref[...] += contract(c, img_next[...], 1, 0)

        @pl.when(s == give_at)
        def _():
            give.start()

        @pl.when(s == take_at)
        def _():
            give.wait_recv()
            gi_ref[...] += gi_in[...]
            give.wait_send()
            to_ahead.wait_send()
            to_behind.wait_send()

            def all_text(b, slot):
                remote(tbuf.at[b], tbuf.at[b], t_send.at[slot], t_recv.at[b, 0], partner).wait_send()

            for _, more, _, own_slot, _ in sides:
                @pl.when(more)
                def _():
                    all_text(chip, own_slot)

            @pl.loop(0, n)
            def _(b):
                @pl.when(((b < chip) & has_right) | ((b > chip) & has_left))
                def _():
                    all_text(b, b)

                @pl.when((b > chip + 1) | (b < chip - 1))
                def _():
                    all_sums(b)

    for side, (_, more, _, _, _) in enumerate(sides):
        @pl.when(more)
        def _():
            all_sums(chip + 1 - 2 * side)


def write_out(gi_ref, gt_ref, gi_out, gt_out, sem):
    part = gi_ref.shape[0] // WRITES
    copies = [
        pltpu.make_async_copy(src.at[pl.ds(w * part, part)], dst.at[pl.ds(w * part, part)], sem.at[m, w])
        for w in range(WRITES)
        for m, (src, dst) in enumerate(((gi_ref, gi_out), (gt_ref, gt_out)))
    ]
    for copy in copies:
        copy.start()
    for copy in copies:
        copy.wait()


def solution(mesh):
    groups, members = mesh.shape["group"], mesh.shape["member"]
    n = members // 2

    def shards(images, texts, sharpness, offset):
        rows, width = images.shape
        tall, count = TALL * rows // PIECES, PIECES // TALL
        bf16 = jnp.bfloat16
        out = jax.ShapeDtypeStruct((rows, width), F32)
        vmem = pl.BlockSpec(memory_space=pltpu.VMEM)
        smem = pl.BlockSpec(memory_space=pltpu.SMEM)
        hbm = pl.BlockSpec(memory_space=pltpu.HBM)
        dma = pltpu.SemaphoreType.DMA
        gi, gt = pl.pallas_call(
            functools.partial(kernel, groups, n),
            out_shape=(out, out),
            in_specs=[smem, smem, hbm, hbm],
            out_specs=(vmem, vmem),
            scratch_shapes=[
                pltpu.VMEM((rows, width), bf16),
                pltpu.VMEM((rows, width), bf16),
                pltpu.VMEM((rows, width), F32),
                pltpu.VMEM((rows, width), F32),
                pltpu.VMEM((rows, width), bf16),
                pltpu.VMEM((rows, width), bf16),
                pltpu.VMEM((n, rows, width), bf16),
                pltpu.VMEM((n, 2, rows, rows), bf16),
                pltpu.VMEM((n + 1, count, tall, width), bf16),
                pltpu.VMEM((n, count, tall, width), bf16),
                pltpu.VMEM((n + 1, count, 1, width), F32),
                pltpu.VMEM((n, count, 1, width), F32),
                dma((n + 1,)),
                dma((n, PIECES)),
                dma((n,)),
                dma((n + 1, count)),
                dma((n,)),
                dma((n + 1, count)),
                dma((4,)),
                dma((4,)),
                dma((2,)),
            ],
            compiler_params=pltpu.CompilerParams(
                collective_id=0, has_side_effects=True, vmem_limit_bytes=min(60, 16 + 3 * n) * 1024 * 1024
            ),
        )(sharpness, offset, *(pltpu.with_memory_space_constraint(a, pltpu.HBM) for a in (images, texts)))
        return pl.pallas_call(
            write_out,
            out_shape=(out, out),
            in_specs=[vmem, vmem],
            out_specs=(hbm, hbm),
            scratch_shapes=[dma((2, WRITES))],
            compiler_params=pltpu.CompilerParams(vmem_limit_bytes=8 * 1024 * 1024),
        )(gi, gt)

    spec = P(("group", "member"), None)
    return jax.shard_map(
        shards, mesh=mesh, in_specs=(spec, spec, P(), P()), out_specs=(spec, spec), check_vma=False
    )
```

```python
import functools

import jax
import jax.numpy as jnp
from jax import lax
from jax.experimental import pallas as pl
from jax.experimental.pallas import tpu as pltpu
from jax.sharding import PartitionSpec as P

MESH = pl.DeviceIdType.MESH
F32 = jnp.float32
PIECES = 8
TALL = 1
WRITES = 4
HOP = 4
AHEAD = 2
LAG = 1


def contract(a, b, da, db):
    return lax.dot_general(a, b, (((da,), (db,)), ((), ())), preferred_element_type=F32)


def order(i, k, n):
    own = jnp.minimum(HOP * k, PIECES)
    j = i - own
    far = (j >= 0) & (j < k * PIECES)
    text_b = jnp.where(far, j // PIECES, k)
    text_p = jnp.where(far, j % PIECES, jnp.where(j < 0, i, i - k * PIECES))
    near = jnp.where(k == 0, HOP, 0)
    i = i - (k + 1) * PIECES
    j, rest = i - near, (n - 2 - k) * PIECES
    far = (j >= 0) & (j < rest)
    sum_b = jnp.where(far, n - 1 - j // PIECES, k + 1)
    sum_p = jnp.where(far, j % PIECES, jnp.where(j < 0, i, i - rest))
    is_text = i < 0
    return is_text, jnp.where(is_text, text_b, sum_b), jnp.where(is_text, text_p, sum_p)


def kernel(
    groups, n, sharp_ref, bias_ref, img_hbm, txt_hbm, gi_ref, gt_ref,
    img_ref, other, gi_other, gi_in, txt_prev, img_next, tbuf, coef, gin, gout, vin, vout,
    t_send, t_recv, g_send, g_recv, v_send, v_recv, x_send, x_recv, l_sem,
):
    rows, width = img_ref.shape
    piece = rows // PIECES
    group = lax.axis_index("group")
    member = lax.axis_index("member")
    chip, core = member // 2, member % 2
    partner = (group, member + 1 - 2 * core)
    ahead = ((group + 1) % groups, member)
    behind = ((group + groups - 1) % groups, member)
    right, left = (group, member + 2), (group, member - 2)
    has_right, has_left = chip + 1 < n, chip > 0

    load_txt = pltpu.make_async_copy(txt_hbm, tbuf.at[chip], l_sem.at[0])
    load_img = pltpu.make_async_copy(img_hbm, img_ref, l_sem.at[1])
    load_txt.start()
    load_img.start()

    barrier = pltpu.get_barrier_semaphore()
    for device in (partner, ahead, behind):
        pl.semaphore_signal(barrier, inc=1, device_id=device, device_id_type=MESH)
    for exists, device in ((has_right, right), (has_left, left)):
        @pl.when(exists)
        def _():
            pl.semaphore_signal(barrier, inc=1, device_id=device, device_id_type=MESH)
    pl.semaphore_wait(barrier, 3 + has_right.astype(jnp.int32) + has_left.astype(jnp.int32))

    def remote(src, dst, send, recv, device):
        return pltpu.make_async_remote_copy(
            src_ref=src, dst_ref=dst, send_sem=send, recv_sem=recv,
            device_id=device, device_id_type=MESH,
        )

    def part_of(p):
        return pl.ds(pl.multiple_of(p * piece, piece), piece)

    def text(b, slot, p, device):
        block = tbuf.at[b, part_of(p)]
        return remote(block, block, t_send.at[slot], t_recv.at[b, p], device)

    def sums(b, slot, p, device):
        return remote(gout.at[b, p], gin.at[slot, p], g_send.at[b], g_recv.at[slot, p], device)

    def means(b, slot, p, device):
        return remote(vout.at[b, p], vin.at[slot, p], v_send.at[b], v_recv.at[slot, p], device)

    swap = remote(img_ref, other, x_send.at[0], x_recv.at[0], partner)
    to_ahead = remote(tbuf.at[chip], txt_prev, x_send.at[1], x_recv.at[1], ahead)
    to_behind = remote(img_ref, img_next, x_send.at[2], x_recv.at[2], behind)
    give = remote(gi_other, gi_in, x_send.at[3], x_recv.at[3], partner)

    sides = (
        (chip, has_right, right, chip, n),
        (n - 1 - chip, has_left, left, n, chip),
    )

    def seen(side, b):
        return b if side == 0 else n - 1 - b

    load_txt.wait()
    for k, more, onward, own_slot, _ in sides:
        @pl.when(more)
        def _():
            for p in range(HOP):
                text(chip, own_slot, p, onward).start()
    load_img.wait()
    swap.start()
    to_ahead.start()
    to_behind.start()
    sharp, bias = sharp_ref[0], bias_ref[0]

    def weights(dots, matching):
        logits = sharp * dots + bias
        if matching:
            hit = lax.broadcasted_iota(jnp.int32, dots.shape, 0) == lax.broadcasted_iota(
                jnp.int32, dots.shape, 1
            )
            sign = jnp.where(hit, 1.0, -1.0).astype(F32)
            return (-sign * (sharp / (1.0 + jnp.exp(sign * logits)))).astype(jnp.bfloat16)
        return (sharp / (1.0 + jnp.exp(-logits))).astype(jnp.bfloat16)

    def weigh(b, part):
        for half, img in ((0, img_ref), (1, other)):
            coef[b, half, part, :] = weights(contract(tbuf[b, part, :], img[...], 1, 1), False)

    def add_images(b):
        for half, total in ((0, gi_ref), (1, gi_other)):
            total[...] += contract(coef[b, half], tbuf[b], 0, 0)

    def tall_part_of(q):
        return pl.ds(pl.multiple_of(q * TALL * piece, TALL * piece), TALL * piece)

    def share(b, q):
        part = tall_part_of(q)
        return contract(coef[b, 0, part, :], img_ref[...], 1, 0) + contract(
            coef[b, 1, part, :], other[...], 1, 0
        )

    def send_on(b, slot, p, total, mean, device):
        middle = jnp.mean(total, axis=0, keepdims=True)
        gout[b, p] = (total - middle).astype(jnp.bfloat16)
        vout[b, p] = middle if mean is None else middle + mean
        sums(b, slot, p, device).start()
        means(b, slot, p, device).start()

    def arrived(slot, p):
        sums(0, slot, p, partner).wait_recv()
        means(0, slot, p, partner).wait_recv()

    own = tbuf.at[chip]
    c = weights(contract(own[...], img_ref[...], 1, 1), True)
    gi_ref[...] = contract(c, own[...], 0, 0)
    gt_ref[...] = contract(c, img_ref[...], 1, 0)
    swap.wait()
    c = weights(contract(own[...], other[...], 1, 1), False)
    gi_other[...] = contract(c, own[...], 0, 0)
    gt_ref[...] += contract(c, other[...], 1, 0)

    def all_sums(b):
        remote(gout.at[b], gout.at[b], g_send.at[b], g_recv.at[b, 0], partner).wait_send()
        remote(vout.at[b], vout.at[b], v_send.at[b], v_recv.at[b, 0], partner).wait_send()

    total_pieces = n * PIECES
    window_at = (n - 1) * PIECES - 8
    give_at = (n - 1) * PIECES + LAG
    take_at = total_pieces - 2

    @pl.loop(0, total_pieces + LAG)
    def _(s):
        for side, (k, more, onward, own_slot, home) in enumerate(sides):
            i, j = s + AHEAD, s - LAG
            out_text, out_b, out_p = order(i, k, n)
            in_text, in_b, in_p = order(j, k - 1, n)
            out_b, in_b = seen(side, out_b), seen(side, in_b)
            going = more & (i < total_pieces)
            coming = (k > 0) & (j >= 0)

            @pl.when(going & out_text & (out_b == chip) & (i >= HOP))
            def _():
                text(chip, own_slot, out_p, onward).start()

            b, p = jnp.where(more, out_b, in_b), jnp.where(more, out_p, in_p)

            @pl.when((going & out_text & (out_b != chip)) | (jnp.logical_not(more) & coming & in_text))
            def _():
                text(b, b, p, onward).wait_recv()

                @pl.when(more)
                def _():
                    text(b, b, p, onward).start()

                weigh(b, part_of(p))

                @pl.when(p == PIECES - 1)
                def _():
                    add_images(b)

            @pl.when(going & jnp.logical_not(out_text) & (out_p % TALL == TALL - 1))
            def _():
                q = out_p // TALL
                arrives_at = chip + 1 - 2 * side
                slot = jnp.where(out_b == arrives_at, n if side == 0 else out_b, out_b)
                here = share(out_b, q)

                @pl.when(k == 0)
                def _():
                    send_on(out_b, slot, q, here, None, onward)

                @pl.when(k > 0)
                def _():
                    arrived(out_b, q)
                    send_on(out_b, slot, q, here + gin[out_b, q].astype(F32), vin[out_b, q], onward)

            @pl.when(coming & jnp.logical_not(in_text) & (in_b == chip) & (in_p % TALL == TALL - 1))
            def _():
                q = in_p // TALL
                arrived(home, q)
                gt_ref[tall_part_of(q), :] += gin[home, q].astype(F32) + vin[home, q]

        @pl.when(s == window_at)
        def _():
            to_ahead.wait_recv()
            c = weights(contract(img_ref[...], txt_prev[...], 1, 1), False)
            gi_ref[...] += contract(c, txt_prev[...], 1, 0)

        @pl.when(s == window_at + 5)
        def _():
            to_behind.wait_recv()
            c = weights(contract(own[...], img_next[...], 1, 1), False)
            gt_ref[...] += contract(c, img_next[...], 1, 0)

        @pl.when(s == give_at)
        def _():
            give.start()

        @pl.when(s == take_at)
        def _():
            give.wait_recv()
            gi_ref[...] += gi_in[...]
            give.wait_send()
            to_ahead.wait_send()
            to_behind.wait_send()

            def all_text(b, slot):
                remote(tbuf.at[b], tbuf.at[b], t_send.at[slot], t_recv.at[b, 0], partner).wait_send()

            for _, more, _, own_slot, _ in sides:
                @pl.when(more)
                def _():
                    all_text(chip, own_slot)

            @pl.loop(0, n)
            def _(b):
                @pl.when(((b < chip) & has_right) | ((b > chip) & has_left))
                def _():
                    all_text(b, b)

                @pl.when((b > chip + 1) | (b < chip - 1))
                def _():
                    all_sums(b)

    for side, (_, more, _, _, _) in enumerate(sides):
        @pl.when(more)
        def _():
            all_sums(chip + 1 - 2 * side)


def write_out(gi_ref, gt_ref, gi_out, gt_out, sem):
    part = gi_ref.shape[0] // WRITES
    copies = [
        pltpu.make_async_copy(src.at[pl.ds(w * part, part)], dst.at[pl.ds(w * part, part)], sem.at[m, w])
        for w in range(WRITES)
        for m, (src, dst) in enumerate(((gi_ref, gi_out), (gt_ref, gt_out)))
    ]
    for copy in copies:
        copy.start()
    for copy in copies:
        copy.wait()


def solution(mesh):
    groups, members = mesh.shape["group"], mesh.shape["member"]
    n = members // 2

    def shards(images, texts, sharpness, offset):
        rows, width = images.shape
        tall, count = TALL * rows // PIECES, PIECES // TALL
        bf16 = jnp.bfloat16
        out = jax.ShapeDtypeStruct((rows, width), F32)
        vmem = pl.BlockSpec(memory_space=pltpu.VMEM)
        smem = pl.BlockSpec(memory_space=pltpu.SMEM)
        hbm = pl.BlockSpec(memory_space=pltpu.HBM)
        dma = pltpu.SemaphoreType.DMA
        gi, gt = pl.pallas_call(
            functools.partial(kernel, groups, n),
            out_shape=(out, out),
            in_specs=[smem, smem, hbm, hbm],
            out_specs=(vmem, vmem),
            scratch_shapes=[
                pltpu.VMEM((rows, width), bf16),
                pltpu.VMEM((rows, width), bf16),
                pltpu.VMEM((rows, width), F32),
                pltpu.VMEM((rows, width), F32),
                pltpu.VMEM((rows, width), bf16),
                pltpu.VMEM((rows, width), bf16),
                pltpu.VMEM((n, rows, width), bf16),
                pltpu.VMEM((n, 2, rows, rows), bf16),
                pltpu.VMEM((n + 1, count, tall, width), bf16),
                pltpu.VMEM((n, count, tall, width), bf16),
                pltpu.VMEM((n + 1, count, 1, width), F32),
                pltpu.VMEM((n, count, 1, width), F32),
                dma((n + 1,)),
                dma((n, PIECES)),
                dma((n,)),
                dma((n + 1, count)),
                dma((n,)),
                dma((n + 1, count)),
                dma((4,)),
                dma((4,)),
                dma((2,)),
            ],
            compiler_params=pltpu.CompilerParams(
                collective_id=0, has_side_effects=True, vmem_limit_bytes=min(60, 16 + 3 * n) * 1024 * 1024
            ),
        )(sharpness, offset, *(pltpu.with_memory_space_constraint(a, pltpu.HBM) for a in (images, texts)))
        return pl.pallas_call(
            write_out,
            out_shape=(out, out),
            in_specs=[vmem, vmem],
            out_specs=(hbm, hbm),
            scratch_shapes=[dma((2, WRITES))],
            compiler_params=pltpu.CompilerParams(vmem_limit_bytes=8 * 1024 * 1024),
        )(gi, gt)

    spec = P(("group", "member"), None)
    return jax.shard_map(
        shards, mesh=mesh, in_specs=(spec, spec, P(), P()), out_specs=(spec, spec), check_vma=False
    )
```

```python
import functools

import jax
import jax.numpy as jnp
from jax import lax
from jax.experimental import pallas as pl
from jax.experimental.pallas import tpu as pltpu
from jax.sharding import PartitionSpec as P

MESH = pl.DeviceIdType.MESH
F32 = jnp.float32
PIECES = 8
TALL = 1
WRITES = 1
HOP = 4
AHEAD = 2
LAG = 1
TAKE_LAG = 2


def contract(a, b, da, db):
    return lax.dot_general(a, b, (((da,), (db,)), ((), ())), preferred_element_type=F32)


def order(i, k, n):
    own = jnp.minimum(HOP * k, PIECES)
    j = i - own
    far = (j >= 0) & (j < k * PIECES)
    text_b = jnp.where(far, j // PIECES, k)
    text_p = jnp.where(far, j % PIECES, jnp.where(j < 0, i, i - k * PIECES))
    near = jnp.where(k == 0, HOP, 0)
    i = i - (k + 1) * PIECES
    j, rest = i - near, (n - 2 - k) * PIECES
    far = (j >= 0) & (j < rest)
    sum_b = jnp.where(far, n - 1 - j // PIECES, k + 1)
    sum_p = jnp.where(far, j % PIECES, jnp.where(j < 0, i, i - rest))
    is_text = i < 0
    return is_text, jnp.where(is_text, text_b, sum_b), jnp.where(is_text, text_p, sum_p)


def kernel(
    groups, n, sharp_ref, bias_ref, img_hbm, txt_hbm, gi_ref, gt_ref,
    img_ref, other, gi_other, gi_in, txt_prev, img_next, tbuf, coef, gin, gout, vin, vout,
    t_send, t_recv, g_send, g_recv, v_send, v_recv, x_send, x_recv, l_sem,
):
    rows, width = img_ref.shape
    piece = rows // PIECES
    group = lax.axis_index("group")
    member = lax.axis_index("member")
    chip, core = member // 2, member % 2
    partner = (group, member + 1 - 2 * core)
    ahead = ((group + 1) % groups, member)
    behind = ((group + groups - 1) % groups, member)
    right, left = (group, member + 2), (group, member - 2)
    has_right, has_left = chip + 1 < n, chip > 0

    load_txt = pltpu.make_async_copy(txt_hbm, tbuf.at[chip], l_sem.at[0])
    load_img = pltpu.make_async_copy(img_hbm, img_ref, l_sem.at[1])
    load_txt.start()
    load_img.start()

    barrier = pltpu.get_barrier_semaphore()
    for device in (partner, ahead, behind):
        pl.semaphore_signal(barrier, inc=1, device_id=device, device_id_type=MESH)
    for exists, device in ((has_right, right), (has_left, left)):
        @pl.when(exists)
        def _():
            pl.semaphore_signal(barrier, inc=1, device_id=device, device_id_type=MESH)
    pl.semaphore_wait(barrier, 3 + has_right.astype(jnp.int32) + has_left.astype(jnp.int32))

    def remote(src, dst, send, recv, device):
        return pltpu.make_async_remote_copy(
            src_ref=src, dst_ref=dst, send_sem=send, recv_sem=recv,
            device_id=device, device_id_type=MESH,
        )

    def part_of(p):
        return pl.ds(pl.multiple_of(p * piece, piece), piece)

    def text(b, slot, p, device):
        block = tbuf.at[b, part_of(p)]
        return remote(block, block, t_send.at[slot], t_recv.at[b, p], device)

    def sums(b, slot, p, device):
        return remote(gout.at[b, p], gin.at[slot, p], g_send.at[b], g_recv.at[slot, p], device)

    def means(b, slot, p, device):
        return remote(vout.at[b, p], vin.at[slot, p], v_send.at[b], v_recv.at[slot, p], device)

    swap = remote(img_ref, other, x_send.at[0], x_recv.at[0], partner)
    to_ahead = remote(tbuf.at[chip], txt_prev, x_send.at[1], x_recv.at[1], ahead)
    to_behind = remote(img_ref, img_next, x_send.at[2], x_recv.at[2], behind)
    give = remote(gi_other, gi_in, x_send.at[3], x_recv.at[3], partner)

    sides = (
        (chip, has_right, right, chip, n),
        (n - 1 - chip, has_left, left, n, chip),
    )

    def seen(side, b):
        return b if side == 0 else n - 1 - b

    load_txt.wait()
    for k, more, onward, own_slot, _ in sides:
        @pl.when(more)
        def _():
            for p in range(HOP):
                text(chip, own_slot, p, onward).start()
    load_img.wait()
    swap.start()
    to_ahead.start()
    to_behind.start()
    sharp, bias = sharp_ref[0], bias_ref[0]

    def weights(dots, matching):
        logits = sharp * dots + bias
        if matching:
            hit = lax.broadcasted_iota(jnp.int32, dots.shape, 0) == lax.broadcasted_iota(
                jnp.int32, dots.shape, 1
            )
            sign = jnp.where(hit, 1.0, -1.0).astype(F32)
            return (-sign * (sharp / (1.0 + jnp.exp(sign * logits)))).astype(jnp.bfloat16)
        return (sharp / (1.0 + jnp.exp(-logits))).astype(jnp.bfloat16)

    def weigh(b, part):
        for half, img in ((0, img_ref), (1, other)):
            coef[b, half, part, :] = weights(contract(tbuf[b, part, :], img[...], 1, 1), False)

    def add_images(b):
        for half, total in ((0, gi_ref), (1, gi_other)):
            total[...] += contract(coef[b, half], tbuf[b], 0, 0)

    def tall_part_of(q):
        return pl.ds(pl.multiple_of(q * TALL * piece, TALL * piece), TALL * piece)

    def share(b, q):
        part = tall_part_of(q)
        return contract(coef[b, 0, part, :], img_ref[...], 1, 0) + contract(
            coef[b, 1, part, :], other[...], 1, 0
        )

    def send_on(b, slot, p, total, mean, device):
        middle = jnp.mean(total, axis=0, keepdims=True)
        gout[b, p] = (total - middle).astype(jnp.bfloat16)
        vout[b, p] = middle if mean is None else middle + mean
        sums(b, slot, p, device).start()
        means(b, slot, p, device).start()

    def arrived(slot, p):
        sums(0, slot, p, partner).wait_recv()
        means(0, slot, p, partner).wait_recv()

    own = tbuf.at[chip]
    c = weights(contract(own[...], img_ref[...], 1, 1), True)
    gi_ref[...] = contract(c, own[...], 0, 0)
    gt_ref[...] = contract(c, img_ref[...], 1, 0)
    swap.wait()
    c = weights(contract(own[...], other[...], 1, 1), False)
    gi_other[...] = contract(c, own[...], 0, 0)
    gt_ref[...] += contract(c, other[...], 1, 0)

    def all_sums(b):
        remote(gout.at[b], gout.at[b], g_send.at[b], g_recv.at[b, 0], partner).wait_send()
        remote(vout.at[b], vout.at[b], v_send.at[b], v_recv.at[b, 0], partner).wait_send()

    total_pieces = n * PIECES
    window_at = (n - 1) * PIECES - 8
    give_at = (n - 1) * PIECES + LAG
    take_at = total_pieces - 2

    @pl.loop(0, total_pieces + TAKE_LAG)
    def _(s):
        for side, (k, more, onward, own_slot, home) in enumerate(sides):
            i, j = s + AHEAD, s - LAG
            out_text, out_b, out_p = order(i, k, n)
            in_text, in_b, in_p = order(j, k - 1, n)
            out_b, in_b = seen(side, out_b), seen(side, in_b)
            going = more & (i < total_pieces)
            coming = (k > 0) & (j >= 0) & (j < total_pieces)
            own_j = s - TAKE_LAG
            own_text, own_b, own_p = order(own_j, k - 1, n)
            own_b = seen(side, own_b)

            @pl.when(going & out_text & (out_b == chip) & (i >= HOP))
            def _():
                text(chip, own_slot, out_p, onward).start()

            b, p = jnp.where(more, out_b, in_b), jnp.where(more, out_p, in_p)

            @pl.when((going & out_text & (out_b != chip)) | (jnp.logical_not(more) & coming & in_text))
            def _():
                text(b, b, p, partner).wait_recv()

                @pl.when(more)
                def _():
                    text(b, b, p, onward).start()

                weigh(b, part_of(p))

                @pl.when(p == PIECES - 1)
                def _():
                    add_images(b)

            @pl.when(going & jnp.logical_not(out_text) & (out_p % TALL == TALL - 1))
            def _():
                q = out_p // TALL
                arrives_at = chip + 1 - 2 * side
                slot = jnp.where(out_b == arrives_at, n if side == 0 else out_b, out_b)
                here = share(out_b, q)

                @pl.when(k == 0)
                def _():
                    send_on(out_b, slot, q, here, None, onward)

                @pl.when(k > 0)
                def _():
                    arrived(out_b, q)
                    send_on(out_b, slot, q, here + gin[out_b, q].astype(F32), vin[out_b, q], onward)

            @pl.when((k > 0) & (own_j >= 0) & jnp.logical_not(own_text) & (own_b == chip) & (own_p % TALL == TALL - 1))
            def _():
                q = own_p // TALL
                arrived(home, q)
                gt_ref[tall_part_of(q), :] += gin[home, q].astype(F32) + vin[home, q]

        @pl.when(s == window_at)
        def _():
            to_ahead.wait_recv()
            c = weights(contract(img_ref[...], txt_prev[...], 1, 1), False)
            gi_ref[...] += contract(c, txt_prev[...], 1, 0)

        @pl.when(s == window_at + 5)
        def _():
            to_behind.wait_recv()
            c = weights(contract(own[...], img_next[...], 1, 1), False)
            gt_ref[...] += contract(c, img_next[...], 1, 0)

        @pl.when(s == give_at)
        def _():
            give.start()

        @pl.when(s == take_at)
        def _():
            give.wait_recv()
            gi_ref[...] += gi_in[...]
            give.wait_send()
            to_ahead.wait_send()
            to_behind.wait_send()

            def all_text(b, slot):
                remote(tbuf.at[b], tbuf.at[b], t_send.at[slot], t_recv.at[b, 0], partner).wait_send()

            for _, more, _, own_slot, _ in sides:
                @pl.when(more)
                def _():
                    all_text(chip, own_slot)

            @pl.loop(0, n)
            def _(b):
                @pl.when(((b < chip) & has_right) | ((b > chip) & has_left))
                def _():
                    all_text(b, b)

                @pl.when((b > chip + 1) | (b < chip - 1))
                def _():
                    all_sums(b)

    for side, (_, more, _, _, _) in enumerate(sides):
        @pl.when(more)
        def _():
            all_sums(chip + 1 - 2 * side)


def write_out(gi_ref, gt_ref, gi_out, gt_out, sem):
    part = gi_ref.shape[0] // WRITES
    copies = [
        pltpu.make_async_copy(src.at[pl.ds(w * part, part)], dst.at[pl.ds(w * part, part)], sem.at[m, w])
        for w in range(WRITES)
        for m, (src, dst) in enumerate(((gi_ref, gi_out), (gt_ref, gt_out)))
    ]
    for copy in copies:
        copy.start()
    for copy in copies:
        copy.wait()


def solution(mesh):
    groups, members = mesh.shape["group"], mesh.shape["member"]
    n = members // 2

    def shards(images, texts, sharpness, offset):
        rows, width = images.shape
        tall, count = TALL * rows // PIECES, PIECES // TALL
        bf16 = jnp.bfloat16
        out = jax.ShapeDtypeStruct((rows, width), F32)
        vmem = pl.BlockSpec(memory_space=pltpu.VMEM)
        smem = pl.BlockSpec(memory_space=pltpu.SMEM)
        hbm = pl.BlockSpec(memory_space=pltpu.HBM)
        dma = pltpu.SemaphoreType.DMA
        gi, gt = pl.pallas_call(
            functools.partial(kernel, groups, n),
            out_shape=(out, out),
            in_specs=[smem, smem, hbm, hbm],
            out_specs=(vmem, vmem),
            scratch_shapes=[
                pltpu.VMEM((rows, width), bf16),
                pltpu.VMEM((rows, width), bf16),
                pltpu.VMEM((rows, width), F32),
                pltpu.VMEM((rows, width), F32),
                pltpu.VMEM((rows, width), bf16),
                pltpu.VMEM((rows, width), bf16),
                pltpu.VMEM((n, rows, width), bf16),
                pltpu.VMEM((n, 2, rows, rows), bf16),
                pltpu.VMEM((n + 1, count, tall, width), bf16),
                pltpu.VMEM((n, count, tall, width), bf16),
                pltpu.VMEM((n + 1, count, 1, width), F32),
                pltpu.VMEM((n, count, 1, width), F32),
                dma((n + 1,)),
                dma((n, PIECES)),
                dma((n,)),
                dma((n + 1, count)),
                dma((n,)),
                dma((n + 1, count)),
                dma((4,)),
                dma((4,)),
                dma((2,)),
            ],
            compiler_params=pltpu.CompilerParams(
                collective_id=0, has_side_effects=True, vmem_limit_bytes=min(60, 16 + 3 * n) * 1024 * 1024
            ),
        )(sharpness, offset, *(pltpu.with_memory_space_constraint(a, pltpu.HBM) for a in (images, texts)))
        return pl.pallas_call(
            write_out,
            out_shape=(out, out),
            in_specs=[vmem, vmem],
            out_specs=(hbm, hbm),
            scratch_shapes=[dma((2, WRITES))],
            compiler_params=pltpu.CompilerParams(vmem_limit_bytes=8 * 1024 * 1024),
        )(gi, gt)

    spec = P(("group", "member"), None)
    return jax.shard_map(
        shards, mesh=mesh, in_specs=(spec, spec, P(), P()), out_specs=(spec, spec), check_vma=False
    )
```

```python
import functools

import jax
import jax.numpy as jnp
from jax import lax
from jax.experimental import pallas as pl
from jax.experimental.pallas import tpu as pltpu
from jax.sharding import PartitionSpec as P

MESH = pl.DeviceIdType.MESH
F32 = jnp.float32
PIECES = 8
TALL = 2
WRITES = 1
HOP = 4
AHEAD = 2
LAG = 1
TAKE_LAG = 3


def contract(a, b, da, db):
    return lax.dot_general(a, b, (((da,), (db,)), ((), ())), preferred_element_type=F32)


def order(i, k, n):
    own = jnp.minimum(HOP * k, PIECES)
    j = i - own
    far = (j >= 0) & (j < k * PIECES)
    text_b = jnp.where(far, j // PIECES, k)
    text_p = jnp.where(far, j % PIECES, jnp.where(j < 0, i, i - k * PIECES))
    near = jnp.where(k == 0, HOP, 0)
    i = i - (k + 1) * PIECES
    j, rest = i - near, (n - 2 - k) * PIECES
    far = (j >= 0) & (j < rest)
    sum_b = jnp.where(far, n - 1 - j // PIECES, k + 1)
    sum_p = jnp.where(far, j % PIECES, jnp.where(j < 0, i, i - rest))
    is_text = i < 0
    return is_text, jnp.where(is_text, text_b, sum_b), jnp.where(is_text, text_p, sum_p)


def kernel(
    groups, n, sharp_ref, bias_ref, img_hbm, txt_hbm, gi_ref, gt_ref,
    img_ref, other, gi_other, gi_in, txt_prev, img_next, tbuf, coef, gin, gout, vin, vout,
    t_send, t_recv, g_send, g_recv, v_send, v_recv, x_send, x_recv, l_sem,
):
    rows, width = img_ref.shape
    piece = rows // PIECES
    group = lax.axis_index("group")
    member = lax.axis_index("member")
    chip, core = member // 2, member % 2
    partner = (group, member + 1 - 2 * core)
    ahead = ((group + 1) % groups, member)
    behind = ((group + groups - 1) % groups, member)
    right, left = (group, member + 2), (group, member - 2)
    has_right, has_left = chip + 1 < n, chip > 0

    load_txt = pltpu.make_async_copy(txt_hbm, tbuf.at[chip], l_sem.at[0])
    load_img = pltpu.make_async_copy(img_hbm, img_ref, l_sem.at[1])
    load_txt.start()
    load_img.start()

    barrier = pltpu.get_barrier_semaphore()
    for device in (partner, ahead, behind):
        pl.semaphore_signal(barrier, inc=1, device_id=device, device_id_type=MESH)
    for exists, device in ((has_right, right), (has_left, left)):
        @pl.when(exists)
        def _():
            pl.semaphore_signal(barrier, inc=1, device_id=device, device_id_type=MESH)
    pl.semaphore_wait(barrier, 3 + has_right.astype(jnp.int32) + has_left.astype(jnp.int32))

    def remote(src, dst, send, recv, device):
        return pltpu.make_async_remote_copy(
            src_ref=src, dst_ref=dst, send_sem=send, recv_sem=recv,
            device_id=device, device_id_type=MESH,
        )

    def part_of(p):
        return pl.ds(pl.multiple_of(p * piece, piece), piece)

    def text(b, slot, p, device):
        block = tbuf.at[b, part_of(p)]
        return remote(block, block, t_send.at[slot], t_recv.at[b, p], device)

    def sums(b, slot, p, device):
        return remote(gout.at[b, p], gin.at[slot, p], g_send.at[b], g_recv.at[slot, p], device)

    def means(b, slot, p, device):
        return remote(vout.at[b, p], vin.at[slot, p], v_send.at[b], v_recv.at[slot, p], device)

    swap = remote(img_ref, other, x_send.at[0], x_recv.at[0], partner)
    to_ahead = remote(tbuf.at[chip], txt_prev, x_send.at[1], x_recv.at[1], ahead)
    to_behind = remote(img_ref, img_next, x_send.at[2], x_recv.at[2], behind)
    give = remote(gi_other, gi_in, x_send.at[3], x_recv.at[3], partner)

    sides = (
        (chip, has_right, right, chip, n),
        (n - 1 - chip, has_left, left, n, chip),
    )

    def seen(side, b):
        return b if side == 0 else n - 1 - b

    load_txt.wait()
    for k, more, onward, own_slot, _ in sides:
        @pl.when(more)
        def _():
            for p in range(HOP):
                text(chip, own_slot, p, onward).start()
    load_img.wait()
    swap.start()
    to_ahead.start()
    to_behind.start()
    sharp, bias = sharp_ref[0], bias_ref[0]

    def weights(dots, matching):
        logits = sharp * dots + bias
        if matching:
            hit = lax.broadcasted_iota(jnp.int32, dots.shape, 0) == lax.broadcasted_iota(
                jnp.int32, dots.shape, 1
            )
            sign = jnp.where(hit, 1.0, -1.0).astype(F32)
            return (-sign * (sharp / (1.0 + jnp.exp(sign * logits)))).astype(jnp.bfloat16)
        return (sharp / (1.0 + jnp.exp(-logits))).astype(jnp.bfloat16)

    def weigh(b, part):
        for half, img in ((0, img_ref), (1, other)):
            coef[b, half, part, :] = weights(contract(tbuf[b, part, :], img[...], 1, 1), False)

    def add_images(b):
        for half, total in ((0, gi_ref), (1, gi_other)):
            total[...] += contract(coef[b, half], tbuf[b], 0, 0)

    def tall_part_of(q):
        return pl.ds(pl.multiple_of(q * TALL * piece, TALL * piece), TALL * piece)

    def share(b, q):
        part = tall_part_of(q)
        return contract(coef[b, 0, part, :], img_ref[...], 1, 0) + contract(
            coef[b, 1, part, :], other[...], 1, 0
        )

    def send_on(b, slot, p, total, mean, device):
        middle = jnp.mean(total, axis=0, keepdims=True)
        gout[b, p] = (total - middle).astype(jnp.bfloat16)
        vout[b, p] = middle if mean is None else middle + mean
        sums(b, slot, p, device).start()
        means(b, slot, p, device).start()

    def arrived(slot, p):
        sums(0, slot, p, partner).wait_recv()
        means(0, slot, p, partner).wait_recv()

    own = tbuf.at[chip]
    c = weights(contract(own[...], img_ref[...], 1, 1), True)
    gi_ref[...] = contract(c, own[...], 0, 0)
    gt_ref[...] = contract(c, img_ref[...], 1, 0)
    swap.wait()
    c = weights(contract(own[...], other[...], 1, 1), False)
    gi_other[...] = contract(c, own[...], 0, 0)
    gt_ref[...] += contract(c, other[...], 1, 0)

    def all_sums(b):
        remote(gout.at[b], gout.at[b], g_send.at[b], g_recv.at[b, 0], partner).wait_send()
        remote(vout.at[b], vout.at[b], v_send.at[b], v_recv.at[b, 0], partner).wait_send()

    total_pieces = n * PIECES
    window_at = (n - 1) * PIECES - 8
    give_at = (n - 1) * PIECES + LAG
    take_at = total_pieces - 2

    @pl.loop(0, total_pieces + TAKE_LAG)
    def _(s):
        for side, (k, more, onward, own_slot, home) in enumerate(sides):
            i, j = s + AHEAD, s - LAG
            out_text, out_b, out_p = order(i, k, n)
            in_text, in_b, in_p = order(j, k - 1, n)
            out_b, in_b = seen(side, out_b), seen(side, in_b)
            going = more & (i < total_pieces)
            coming = (k > 0) & (j >= 0) & (j < total_pieces)
            own_j = s - TAKE_LAG
            own_text, own_b, own_p = order(own_j, k - 1, n)
            own_b = seen(side, own_b)

            @pl.when(going & out_text & (out_b == chip) & (i >= HOP))
            def _():
                text(chip, own_slot, out_p, onward).start()

            b, p = jnp.where(more, out_b, in_b), jnp.where(more, out_p, in_p)

            @pl.when((going & out_text & (out_b != chip)) | (jnp.logical_not(more) & coming & in_text))
            def _():
                text(b, b, p, partner).wait_recv()

                @pl.when(more)
                def _():
                    text(b, b, p, onward).start()

                weigh(b, part_of(p))

                @pl.when(p == PIECES - 1)
                def _():
                    add_images(b)

            @pl.when(going & jnp.logical_not(out_text) & (out_p % TALL == TALL - 1))
            def _():
                q = out_p // TALL
                arrives_at = chip + 1 - 2 * side
                slot = jnp.where(out_b == arrives_at, n if side == 0 else out_b, out_b)
                here = share(out_b, q)

                @pl.when(k == 0)
                def _():
                    send_on(out_b, slot, q, here, None, onward)

                @pl.when(k > 0)
                def _():
                    arrived(out_b, q)
                    send_on(out_b, slot, q, here + gin[out_b, q].astype(F32), vin[out_b, q], onward)

            @pl.when((k > 0) & (own_j >= 0) & jnp.logical_not(own_text) & (own_b == chip) & (own_p % TALL == TALL - 1))
            def _():
                q = own_p // TALL
                arrived(home, q)
                gt_ref[tall_part_of(q), :] += gin[home, q].astype(F32) + vin[home, q]

        @pl.when(s == window_at)
        def _():
            to_ahead.wait_recv()
            c = weights(contract(img_ref[...], txt_prev[...], 1, 1), False)
            gi_ref[...] += contract(c, txt_prev[...], 1, 0)

        @pl.when(s == window_at + 5)
        def _():
            to_behind.wait_recv()
            c = weights(contract(own[...], img_next[...], 1, 1), False)
            gt_ref[...] += contract(c, img_next[...], 1, 0)

        @pl.when(s == give_at)
        def _():
            give.start()

        @pl.when(s == take_at)
        def _():
            give.wait_recv()
            gi_ref[...] += gi_in[...]
            give.wait_send()
            to_ahead.wait_send()
            to_behind.wait_send()

            def all_text(b, slot):
                remote(tbuf.at[b], tbuf.at[b], t_send.at[slot], t_recv.at[b, 0], partner).wait_send()

            for _, more, _, own_slot, _ in sides:
                @pl.when(more)
                def _():
                    all_text(chip, own_slot)

            @pl.loop(0, n)
            def _(b):
                @pl.when(((b < chip) & has_right) | ((b > chip) & has_left))
                def _():
                    all_text(b, b)

                @pl.when((b > chip + 1) | (b < chip - 1))
                def _():
                    all_sums(b)

    for side, (_, more, _, _, _) in enumerate(sides):
        @pl.when(more)
        def _():
            all_sums(chip + 1 - 2 * side)


def write_out(gi_ref, gt_ref, gi_out, gt_out, sem):
    part = gi_ref.shape[0] // WRITES
    copies = [
        pltpu.make_async_copy(src.at[pl.ds(w * part, part)], dst.at[pl.ds(w * part, part)], sem.at[m, w])
        for w in range(WRITES)
        for m, (src, dst) in enumerate(((gi_ref, gi_out), (gt_ref, gt_out)))
    ]
    for copy in copies:
        copy.start()
    for copy in copies:
        copy.wait()


def solution(mesh):
    groups, members = mesh.shape["group"], mesh.shape["member"]
    n = members // 2

    def shards(images, texts, sharpness, offset):
        rows, width = images.shape
        tall, count = TALL * rows // PIECES, PIECES // TALL
        bf16 = jnp.bfloat16
        out = jax.ShapeDtypeStruct((rows, width), F32)
        vmem = pl.BlockSpec(memory_space=pltpu.VMEM)
        smem = pl.BlockSpec(memory_space=pltpu.SMEM)
        hbm = pl.BlockSpec(memory_space=pltpu.HBM)
        dma = pltpu.SemaphoreType.DMA
        gi, gt = pl.pallas_call(
            functools.partial(kernel, groups, n),
            out_shape=(out, out),
            in_specs=[smem, smem, hbm, hbm],
            out_specs=(vmem, vmem),
            scratch_shapes=[
                pltpu.VMEM((rows, width), bf16),
                pltpu.VMEM((rows, width), bf16),
                pltpu.VMEM((rows, width), F32),
                pltpu.VMEM((rows, width), F32),
                pltpu.VMEM((rows, width), bf16),
                pltpu.VMEM((rows, width), bf16),
                pltpu.VMEM((n, rows, width), bf16),
                pltpu.VMEM((n, 2, rows, rows), bf16),
                pltpu.VMEM((n + 1, count, tall, width), bf16),
                pltpu.VMEM((n, count, tall, width), bf16),
                pltpu.VMEM((n + 1, count, 1, width), F32),
                pltpu.VMEM((n, count, 1, width), F32),
                dma((n + 1,)),
                dma((n, PIECES)),
                dma((n,)),
                dma((n + 1, count)),
                dma((n,)),
                dma((n + 1, count)),
                dma((4,)),
                dma((4,)),
                dma((2,)),
            ],
            compiler_params=pltpu.CompilerParams(
                collective_id=0, has_side_effects=True, vmem_limit_bytes=min(60, 16 + 3 * n) * 1024 * 1024
            ),
        )(sharpness, offset, *(pltpu.with_memory_space_constraint(a, pltpu.HBM) for a in (images, texts)))
        return pl.pallas_call(
            write_out,
            out_shape=(out, out),
            in_specs=[vmem, vmem],
            out_specs=(hbm, hbm),
            scratch_shapes=[dma((2, WRITES))],
            compiler_params=pltpu.CompilerParams(vmem_limit_bytes=8 * 1024 * 1024),
        )(gi, gt)

    spec = P(("group", "member"), None)
    return jax.shard_map(
        shards, mesh=mesh, in_specs=(spec, spec, P(), P()), out_specs=(spec, spec), check_vma=False
    )
```
